32 devices in a mesh: groups: 2 (over x), view: 16 (over z, y, core).
Axes of the slice: x: 2, y: 2, z: 4, core: 2. Of those that a mesh axis runs over, the one named last changes fastest.
Arguments:
- materials: float32 [3, 64, 256, 512], P(None, ('groups', 'view')), parts along dimension 1, as said below
- column_profile: bfloat16 [2, 512, 1280], replicated, as said below
- row_profile: bfloat16 [2, 256, 1280], replicated, as said below
- start_block: int32 [32], P(('groups', 'view')), parts along dimension 0, may hold values from 0 to 30, as said below
- block_count: int32 [32], P(('groups', 'view')), parts along dimension 0, may hold values from 1 to 4, as said below
- tile_ids: int32 [32, 4], P(('groups', 'view')), parts along dimension 0, may hold values from 0 to 1
- photon_counts: int32 [32, 8, 4, 1280], P(('groups', 'view')), parts along dimension 0, may hold values from 0 to 3199
- spectrum: float32 [8, 16], replicated, may hold values from 20 to 200
- attenuation: float32 [16, 3], replicated, may hold values from 0.05 to 0.5
- step_size: float32 [3], replicated, may hold values from 0.002 to 0.01
Outputs:
- updated: float32 [3, 64, 256, 512], P(None, ('groups', 'view')), parts along dimension 1
The draws below stay inside these ranges and needn't reach their ends.
There are 2 independent parts, one for each index of `groups`. The reference program is written for one: setup_inputs(seed, part) draws one part's arguments, and reference() takes and returns one part's arrays. A program takes and returns all parts, laid end to end along the dimension named above; an argument that names none is the same for every part. Nothing has to cross between parts.
Inputs may be any that keep to these rules, and one draw needn't show every extreme that they name: `start_block`: every slice of a view's window lies among the 2 slices of the device that holds the view (view v belongs to device v) and the 2 slices on either side; the window ends at or before slice 32 - 1. `block_count`: windows of views are ragged; some view of every scan covers 4 slices. `column_profile`: entries are non-negative and below 1. `row_profile`: entries are non-negative and below 1. `materials`: entries lie between 0 and 1.
All inputs are finite; a program needn't handle non-finite values.
Results may differ from the reference program's by a relative error of at most 0.00057.
Values may be sent and summed in bfloat16 or wider, within the bound.
A program may use at most 64 MiB of HBM per device.

```python
import math
import jax
import jax.numpy as jnp
from jax import lax

M = 3
E = 8
K = 16
PIX = 1280
SX = 512
SY = 256
WMAX = 4
VPD = 1
BLK_DEV = 2
NT = 2
ITERS = 2
DROWS = 4
NB = 32
VIEWS = 16
N_VIEW = 16


def window_pair(key):
    key_offset, key_count = jax.random.split(jax.random.fold_in(key, 4242))
    views = jnp.arange(VIEWS).astype(jnp.int32)
    owner = views // VPD
    offset = jax.random.randint(key_offset, (VIEWS,), -BLK_DEV, 2 * BLK_DEV - WMAX + 1).astype(jnp.int32)
    number = jax.random.randint(key_count, (VIEWS,), 1, WMAX + 1).astype(jnp.int32)
    number = jnp.where(views == 2 * VPD, 1, number)
    reach_down = (views == VIEWS - 1) | (views == VPD)
    reach_up = (views == 0) | (views == (N_VIEW - 1) * VPD - 1)
    offset = jnp.where(reach_down, -BLK_DEV, offset)
    offset = jnp.where(reach_up, 2 * BLK_DEV - WMAX, offset)
    number = jnp.where(reach_down | reach_up, WMAX, number)
    first = jnp.maximum(owner * BLK_DEV + offset, 0)
    last = jnp.minimum(first + number, NB)
    return (first.astype(jnp.int32), (last - first).astype(jnp.int32))


def draw_start_block(key, part):
    return window_pair(key)[0]


def draw_block_count(key, part):
    return window_pair(key)[1]


def banded(key, rows, width, centers):
    positions = jnp.arange(rows).astype(jnp.int32)[None, :, None]
    distance = (positions - centers[:, None, :] + width // 2) % rows
    inside = (distance < width).astype(jnp.float32)
    values = jax.random.uniform(jax.random.fold_in(key, 77), (NT, rows, PIX), jnp.float32, 0.5, 1.5)
    return (inside * values / width).astype(jnp.bfloat16)


def draw_column_profile(key, part):
    detector = jnp.arange(PIX).astype(jnp.int32)[None, :]
    tiles = jnp.arange(NT).astype(jnp.int32)[:, None]
    centers = (detector * SX // PIX + tiles * (SX // 7)) % SX
    return banded(jax.random.fold_in(key, 11), SX, max(SX // 32, 4), centers)


def draw_row_profile(key, part):
    detector = jnp.arange(PIX).astype(jnp.int32)[None, :]
    tiles = jnp.arange(NT).astype(jnp.int32)[:, None]
    centers = (detector * 37 + tiles * (SY // 3)) % SY
    return banded(jax.random.fold_in(key, 13), SY, max(SY // 8, 4), centers)


def draw_materials(key, part):
    key_level, key_factor = jax.random.split(jax.random.fold_in(key, 909))
    levels = jax.random.uniform(key_level, (M, NB, 8, 16), jnp.float32, 0.05, 1.0)
    factor = jax.random.uniform(key_factor, (M, NB, SY, SX), jnp.float32, 0.5, 1.0)
    blocky = jnp.repeat(jnp.repeat(levels, SY // 8, axis=2), SX // 16, axis=3)
    return blocky * factor


def with_ends(values, own_key, least, largest):
    longest = values.shape.index(max(values.shape))
    spots = []
    for shift in (0, 1):
        where = [jax.random.randint(jax.random.fold_in(own_key, axis), (), 0, length) for axis, length in enumerate(values.shape)]
        where[longest] = (where[longest] + shift) % values.shape[longest]
        spots.append(tuple(where))
    return values.at[spots[0]].set(least).at[spots[1]].set(largest)


def setup_inputs(seed: int = 0, part: int = 0) -> dict:
    key_of = jax.random.split(jax.random.key(seed), 11)
    part_splits = jax.random.split(jax.random.fold_in(key_of[10], part), 11)
    return {
        "materials": draw_materials(jax.random.fold_in(jax.random.fold_in(key_of[10], part), 71), part),
        "column_profile": draw_column_profile(jax.random.fold_in(key_of[10], 71), part),
        "row_profile": draw_row_profile(jax.random.fold_in(key_of[10], 71), part),
        "start_block": draw_start_block(jax.random.fold_in(jax.random.fold_in(key_of[10], part), 71), part),
        "block_count": draw_block_count(jax.random.fold_in(jax.random.fold_in(key_of[10], part), 71), part),
        "tile_ids": with_ends(jax.random.randint(part_splits[5], (VIEWS, WMAX), 0, NT), jax.random.fold_in(part_splits[5], 1), 0, NT - 1).astype(jnp.int32),
        "photon_counts": with_ends(jax.random.randint(part_splits[6], (VIEWS, E, DROWS, PIX), 0, 3200), jax.random.fold_in(part_splits[6], 1), 0, 3199).astype(jnp.int32),
        "spectrum": jnp.clip(jnp.exp(jax.random.uniform(key_of[7], (E, K), jnp.float32, math.log(20.0), math.log(200.0))), 20.0, 200.0),
        "attenuation": jnp.clip(jnp.exp(jax.random.uniform(key_of[8], (K, M), jnp.float32, math.log(0.05), math.log(0.5))), 0.05, 0.5),
        "step_size": jnp.clip(jnp.exp(jax.random.uniform(key_of[9], (M,), jnp.float32, math.log(0.002), math.log(0.01))), 0.002, 0.01),
    }


def poisson_gradient(line, counts, rowmask, spectrum, attenuation):
    highest = lax.Precision.HIGHEST
    atten_sum = jnp.einsum("km,vmrp->vkrp", attenuation, line, precision=highest)
    trans = jnp.exp(-atten_sum)
    expected = jnp.einsum("ek,vkrp->verp", spectrum, trans, precision=highest)
    weight = 1.0 - counts.astype(jnp.float32) / expected
    back_terms = jnp.einsum("ek,verp->vkrp", spectrum, weight, precision=highest)
    grad_full = -jnp.einsum("km,vkrp->vmrp", attenuation, trans * back_terms, precision=highest)
    return (grad_full * rowmask[:, None, :, None]).astype(jnp.bfloat16)


def reference(materials, column_profile, row_profile, start_block, block_count, tile_ids, photon_counts, spectrum, attenuation, step_size):
    row_slot = jnp.arange(DROWS).astype(jnp.int32)
    for iteration in range(ITERS):
        rounded = materials.astype(jnp.bfloat16)

        def view_step(summed, inputs):
            first, number, tiles_here, counts = inputs
            pieces = []
            for slot_index in range(WMAX):
                block_index = jnp.clip(first + slot_index, 0, NB - 1).astype(jnp.int32)
                valid = (slot_index < number).astype(jnp.float32)
                block_data = lax.dynamic_index_in_dim(rounded, block_index, 1, keepdims=False)
                col_tile = lax.dynamic_index_in_dim(column_profile, tiles_here[slot_index], 0, keepdims=False)
                row_tile = lax.dynamic_index_in_dim(row_profile, tiles_here[slot_index], 0, keepdims=False)
                across = jnp.dot(block_data.reshape(M * SY, SX), col_tile, preferred_element_type=jnp.float32).reshape(M, SY, PIX)
                piece = jnp.sum(across * row_tile.astype(jnp.float32)[None], axis=1)
                pieces.append(piece * valid)
            line = jnp.stack(pieces, axis=1)
            rowmask = (row_slot < number).astype(jnp.float32)
            gradient = poisson_gradient(line[None], counts[None], rowmask[None], spectrum, attenuation)[0]
            for slot_index in range(WMAX):
                block_index = jnp.clip(first + slot_index, 0, NB - 1).astype(jnp.int32)
                valid = (slot_index < number).astype(jnp.float32)
                col_tile = lax.dynamic_index_in_dim(column_profile, tiles_here[slot_index], 0, keepdims=False)
                row_tile = lax.dynamic_index_in_dim(row_profile, tiles_here[slot_index], 0, keepdims=False)
                grad_rows = gradient[:, slot_index, :].astype(jnp.float32)
                weighted = (grad_rows[:, None, :] * row_tile.astype(jnp.float32)[None]).astype(jnp.bfloat16)
                contrib = lax.dot_general(weighted.reshape(M * SY, PIX), col_tile, (((1,), (1,)), ((), ())), preferred_element_type=jnp.float32)
                current = lax.dynamic_index_in_dim(summed, block_index, 1, keepdims=False)
                summed = lax.dynamic_update_index_in_dim(summed, current + valid * contrib.reshape(M, SY, SX), block_index, 1)
            return summed, None

        zeros = jnp.zeros(materials.shape, jnp.float32)
        backprojected, unused = lax.scan(view_step, zeros, (start_block, block_count, tile_ids, photon_counts))
        materials = materials - step_size[:, None, None, None] * backprojected
    return materials
```

```python
import functools

import jax
import jax.numpy as jnp
from jax import lax
from jax.experimental import pallas as pl
from jax.experimental.pallas import tpu as pltpu
from jax.sharding import PartitionSpec as P

ITERS = 2
MESH = pl.DeviceIdType.MESH
F32 = jnp.float32
BF16 = jnp.bfloat16


def kernel(
    n,
    start_ref,
    count_ref,
    tiles_ref,
    spec_ref,
    atten_ref,
    step_ref,
    mats_ref,
    col_ref,
    row_ref,
    counts_ref,
    out_ref,
    rounded,
    lines,
    line_rows,
    line_pack,
    count_pack,
    grad_pack,
    grad_rows,
    grad_send,
    grad_recv,
    grad_sum,
    line_send_sem,
    line_recv_sem,
    grad_send_sem,
    grad_recv_sem,
):
    me = lax.axis_index("view")
    mats, own, height, width = mats_ref.shape
    tiles, _, columns = col_ref.shape
    window = tiles_ref.shape[1]
    bins, energies = spec_ref.shape
    pairs = own * tiles
    half = columns // 2
    has_low, has_high = me > 0, me < n - 1
    low, high = jnp.maximum(me - 1, 0), jnp.minimum(me + 1, n - 1)

    barrier = pltpu.get_barrier_semaphore()

    @pl.when(has_low)
    def _():
        pl.semaphore_signal(barrier, inc=1, device_id={"view": low}, device_id_type=MESH)

    @pl.when(has_high)
    def _():
        pl.semaphore_signal(barrier, inc=1, device_id={"view": high}, device_id_type=MESH)

    @pl.when(jnp.logical_not(has_low))
    def _():
        for it in range(ITERS):
            grad_recv[it, 0] = jnp.zeros(grad_recv.shape[2:], BF16)
            lines[it, 0:pairs] = jnp.zeros((pairs, mats, columns), F32)

    @pl.when(jnp.logical_not(has_high))
    def _():
        for it in range(ITERS):
            grad_recv[it, 1] = jnp.zeros(grad_recv.shape[2:], BF16)
            lines[it, 2 * pairs : 3 * pairs] = jnp.zeros((pairs, mats, columns), F32)

    def line_copy(it, way, s):
        landing = 0 if way == 0 else 2 * pairs
        return pltpu.make_async_remote_copy(
            src_ref=lines.at[it, pl.ds(pairs + s * tiles, tiles)],
            dst_ref=lines.at[it, pl.ds(landing + s * tiles, tiles)],
            send_sem=line_send_sem.at[it, way, s],
            recv_sem=line_recv_sem.at[it, way, s],
            device_id={"view": high if way == 0 else low},
            device_id_type=MESH,
        )

    def grad_copy(it, way):
        leaving = 2 * pairs if way == 0 else 0
        return pltpu.make_async_remote_copy(
            src_ref=grad_send.at[it, pl.ds(leaving, pairs)],
            dst_ref=grad_recv.at[it, way],
            send_sem=grad_send_sem.at[it, way],
            recv_sem=grad_recv_sem.at[it, way],
            device_id={"view": high if way == 0 else low},
            device_id_type=MESH,
        )

    sends = ((0, has_high), (1, has_low))
    receives = ((0, has_low), (1, has_high))

    for e in range(bins):
        c = counts_ref[0, e].astype(F32)
        count_pack[e] = jnp.concatenate([c[:, :half], c[:, half:]], axis=0)

    for s in range(own):
        for m in range(mats):
            rounded[s, m] = mats_ref[m, s].astype(BF16)

    first = start_ref[0] - (me * own - own)
    number = count_ref[0]

    for it in range(ITERS):
        for s in range(own):

            def chunk(i, _, s=s):
                cols = pl.ds(pl.multiple_of(i * 256, 256), 256)
                block = rounded[s].reshape(mats * height, width)
                for t in range(tiles):
                    across = jnp.dot(block, col_ref[t, :, cols], preferred_element_type=F32)
                    across = across.reshape(mats, height, 256) * row_ref[t, :, cols].astype(F32)[None]
                    lines[it, pairs + s * tiles + t, :, cols] = jnp.sum(across, axis=1)
                return 0

            lax.fori_loop(0, columns // 256, chunk, 0)
            if it == 0 and s == 0:
                pl.semaphore_wait(barrier, has_low.astype(jnp.int32) + has_high.astype(jnp.int32))

            for way, there in sends:

                @pl.when(there)
                def _(way=way, s=s):
                    line_copy(it, way, s).start()

        for s in range(own):
            for way, there in receives:

                @pl.when(there)
                def _(way=way, s=s):
                    line_copy(it, way, s).wait_recv()

        for j in range(window):
            at = jnp.clip(first + j, 0, 3 * own - 1) * tiles + tiles_ref[0, j]
            line_rows[j] = jnp.where(j < number, lines[it, at], 0.0)
        for m in range(mats):
            x = line_rows[:, m, :]
            line_pack[m] = jnp.concatenate([x[:, :half], x[:, half:]], axis=0)

        def poisson(i, _):
            cols = pl.ds(pl.multiple_of(i * 128, 128), 128)
            xs = [line_pack[m, :, cols] for m in range(mats)]
            trans = []
            for k in range(energies):
                total = atten_ref[k, 0] * xs[0]
                for m in range(1, mats):
                    total = total + atten_ref[k, m] * xs[m]
                trans.append(jnp.exp(-total))
            back = [None] * energies
            for e in range(bins):
                expected = spec_ref[e, 0] * trans[0]
                for k in range(1, energies):
                    expected = expected + spec_ref[e, k] * trans[k]
                weight = 1.0 - count_pack[e, :, cols] / expected
                for k in range(energies):
                    term = spec_ref[e, k] * weight
                    back[k] = term if e == 0 else back[k] + term
            for m in range(mats):
                total = None
                for k in range(energies):
                    term = atten_ref[k, m] * (trans[k] * back[k])
                    total = term if k == 0 else total + term
                grad_pack[m, :, cols] = -total
            return 0

        lax.fori_loop(0, half // 128, poisson, 0)
        for m in range(mats):
            y = grad_pack[m]
            grad_rows[:, m, :] = jnp.concatenate([y[:window], y[window:]], axis=1)
        for place in list(range(own)) + list(range(2 * own, 3 * own)) + list(range(own, 2 * own)):
            j = place - first
            held = (j >= 0) & (j < number)
            j = jnp.clip(j, 0, window - 1)
            value = grad_rows[j]
            tile = tiles_ref[0, j]
            for t in range(tiles):
                grad_send[it, place * tiles + t] = jnp.where(held & (tile == t), value, 0.0).astype(BF16)
        for way, there in sends:

            @pl.when(there)
            def _(way=way):
                grad_copy(it, way).start()

        for way, there in receives:

            @pl.when(there)
            def _(way=way):
                grad_copy(it, way).wait_recv()

        grad_sum[...] = (
            grad_send[it, pairs : 2 * pairs].astype(F32)
            + grad_recv[it, 0].astype(F32)
            + grad_recv[it, 1].astype(F32)
        )

        before = mats_ref if it == 0 else out_ref

        def back_step(s, _):
            for m in range(mats):
                total = None
                for t in range(tiles):
                    g = grad_sum[s * tiles + t][m : m + 1]
                    weighted = (g * row_ref[t].astype(F32)).astype(BF16)
                    part = lax.dot_general(
                        weighted, col_ref[t], (((1,), (1,)), ((), ())), preferred_element_type=F32
                    )
                    total = part if t == 0 else total + part
                new = before[m, s] - step_ref[m] * total
                out_ref[m, s] = new
                if it < ITERS - 1:
                    rounded[s, m] = new.astype(BF16)
            return 0

        lax.fori_loop(0, own, back_step, 0)

    for it in range(ITERS):
        for way, there in sends:

            @pl.when(there)
            def _(way=way, it=it):
                for s in range(own):
                    line_copy(it, way, s).wait_send()
                grad_copy(it, way).wait_send()


def solution(mesh):
    n = mesh.shape["view"]

    def local(materials, column_profile, row_profile, start, count, tile_ids, counts, spectrum, attenuation, step):
        mats, own, height, width = materials.shape
        tiles, _, columns = column_profile.shape
        views, window = tile_ids.shape
        bins = spectrum.shape[0]
        assert views == 1
        pairs = own * tiles
        vmem = pl.BlockSpec(memory_space=pltpu.VMEM)
        smem = pl.BlockSpec(memory_space=pltpu.SMEM)
        return pl.pallas_call(
            functools.partial(kernel, n),
            out_shape=jax.ShapeDtypeStruct(materials.shape, F32),
            in_specs=[smem] * 6 + [vmem] * 4,
            out_specs=vmem,
            scratch_shapes=[
                pltpu.VMEM((own, mats, height, width), BF16),
                pltpu.VMEM((ITERS, 3 * pairs, mats, columns), F32),
                pltpu.VMEM((window, mats, columns), F32),
                pltpu.VMEM((mats, 2 * window, columns // 2), F32),
                pltpu.VMEM((bins, 2 * window, columns // 2), F32),
                pltpu.VMEM((mats, 2 * window, columns // 2), F32),
                pltpu.VMEM((window, mats, columns), F32),
                pltpu.VMEM((ITERS, 3 * pairs, mats, columns), BF16),
                pltpu.VMEM((ITERS, 2, pairs, mats, columns), BF16),
                pltpu.VMEM((pairs, mats, columns), F32),
                pltpu.SemaphoreType.DMA((ITERS, 2, own)),
                pltpu.SemaphoreType.DMA((ITERS, 2, own)),
                pltpu.SemaphoreType.DMA((ITERS, 2)),
                pltpu.SemaphoreType.DMA((ITERS, 2)),
            ],
            compiler_params=pltpu.CompilerParams(
                collective_id=0, has_side_effects=True, vmem_limit_bytes=56 * 1024 * 1024
            ),
        )(start, count, tile_ids, spectrum, attenuation, step, materials, column_profile, row_profile, counts)

    placed = (
        P(None, ("groups", "view"), None, None),
        P(),
        P(),
        P(("groups", "view")),
        P(("groups", "view")),
        P(("groups", "view"), None),
        P(("groups", "view"), None, None, None),
        P(),
        P(),
        P(),
    )
    return jax.shard_map(
        local,
        mesh=mesh,
        in_specs=placed,
        out_specs=P(None, ("groups", "view"), None, None),
        check_vma=False,
    )
```

```python
import functools

import jax
import jax.numpy as jnp
from jax import lax
from jax.experimental import pallas as pl
from jax.experimental.pallas import tpu as pltpu
from jax.sharding import PartitionSpec as P

ITERS = 2
MESH = pl.DeviceIdType.MESH
F32 = jnp.float32
BF16 = jnp.bfloat16


def back_projected(mats, tiles, s, grad_ref, row_ref, col_ref):
    total = None
    for t in range(tiles):
        g = grad_ref[s * tiles + t]
        profile = row_ref[t].astype(F32)
        weighted = jnp.concatenate([(g[m : m + 1] * profile).astype(BF16) for m in range(mats)], axis=0)
        part = lax.dot_general(weighted, col_ref[t], (((1,), (1,)), ((), ())), preferred_element_type=F32)
        total = part if t == 0 else total + part
    return total


def final_kernel(step_ref, grad_ref, col_ref, row_ref, mats_ref, out_ref):
    mats, _, height, _ = mats_ref.shape
    total = back_projected(mats, col_ref.shape[0], pl.program_id(0), grad_ref, row_ref, col_ref)
    for m in range(mats):
        out_ref[m, 0] = mats_ref[m, 0] - step_ref[m] * total[m * height : (m + 1) * height]


def kernel(
    n,
    start_ref,
    count_ref,
    tiles_ref,
    spec_ref,
    atten_ref,
    step_ref,
    mats_ref,
    col_ref,
    row_ref,
    counts_ref,
    grad_sum,
    mats_out,
    maps,
    column,
    row,
    rounded,
    lines,
    line_rows,
    line_pack,
    count_pack,
    grad_pack,
    grad_rows,
    grad_send,
    grad_recv,
    load_sem,
    chunk_sem,
    store_sem,
    line_send_sem,
    line_recv_sem,
    grad_send_sem,
    grad_recv_sem,
):
    me = lax.axis_index("view")
    mats, own, height, width = mats_ref.shape
    tiles, _, columns = col_ref.shape
    window = tiles_ref.shape[1]
    bins, energies = spec_ref.shape
    pairs = own * tiles
    half = columns // 2
    has_low, has_high = me > 0, me < n - 1
    low, high = jnp.maximum(me - 1, 0), jnp.minimum(me + 1, n - 1)

    def maps_load(s):
        return pltpu.make_async_copy(mats_ref.at[:, s], maps.at[s], load_sem.at[s])

    def chunk_load(which, i):
        cols = pl.ds(pl.multiple_of(i * 256, 256), 256)
        source, target = ((col_ref, column), (row_ref, row))[which]
        return pltpu.make_async_copy(source.at[:, :, cols], target.at[:, :, cols], chunk_sem.at[which, i])

    def maps_store(s):
        return pltpu.make_async_copy(maps.at[s], mats_out.at[:, s], store_sem.at[s])

    maps_load(0).start()
    for i in range(columns // 256):
        chunk_load(0, i).start()
        chunk_load(1, i).start()
    for s in range(1, own):
        maps_load(s).start()

    barrier = pltpu.get_barrier_semaphore()

    @pl.when(has_low)
    def _():
        pl.semaphore_signal(barrier, inc=1, device_id={"view": low}, device_id_type=MESH)

    @pl.when(has_high)
    def _():
        pl.semaphore_signal(barrier, inc=1, device_id={"view": high}, device_id_type=MESH)

    @pl.when(jnp.logical_not(has_low))
    def _():
        for it in range(ITERS):
            grad_recv[it, 0] = jnp.zeros(grad_recv.shape[2:], BF16)
            lines[it, 0:pairs] = jnp.zeros((pairs, mats, columns), F32)

    @pl.when(jnp.logical_not(has_high))
    def _():
        for it in range(ITERS):
            grad_recv[it, 1] = jnp.zeros(grad_recv.shape[2:], BF16)
            lines[it, 2 * pairs : 3 * pairs] = jnp.zeros((pairs, mats, columns), F32)

    def line_copy(it, way, s):
        landing = 0 if way == 0 else 2 * pairs
        return pltpu.make_async_remote_copy(
            src_ref=lines.at[it, pl.ds(pairs + s * tiles, tiles)],
            dst_ref=lines.at[it, pl.ds(landing + s * tiles, tiles)],
            send_sem=line_send_sem.at[it, way, s],
            recv_sem=line_recv_sem.at[it, way, s],
            device_id={"view": high if way == 0 else low},
            device_id_type=MESH,
        )

    def grad_copy(it, way):
        leaving = 2 * pairs if way == 0 else 0
        return pltpu.make_async_remote_copy(
            src_ref=grad_send.at[it, pl.ds(leaving, pairs)],
            dst_ref=grad_recv.at[it, way],
            send_sem=grad_send_sem.at[it, way],
            recv_sem=grad_recv_sem.at[it, way],
            device_id={"view": high if way == 0 else low},
            device_id_type=MESH,
        )

    sends = ((0, has_high), (1, has_low))
    receives = ((0, has_low), (1, has_high))

    for e in range(bins):
        c = counts_ref[0, e].astype(F32)
        count_pack[e] = jnp.concatenate([c[:, :half], c[:, half:]], axis=0)

    first = start_ref[0] - (me * own - own)
    number = count_ref[0]

    for it in range(ITERS):
        for s in range(own):
            if it == 0:
                maps_load(s).wait()
                for m in range(mats):
                    rounded[s, m] = maps[s, m].astype(BF16)

            def chunk(i, _, s=s):
                if it == 0 and s == 0:
                    chunk_load(0, i).wait()
                    chunk_load(1, i).wait()
                cols = pl.ds(pl.multiple_of(i * 256, 256), 256)
                block = rounded[s].reshape(mats * height, width)
                for t in range(tiles):
                    across = jnp.dot(block, column[t, :, cols], preferred_element_type=F32)
                    across = across.reshape(mats, height, 256) * row[t, :, cols].astype(F32)[None]
                    lines[it, pairs + s * tiles + t, :, cols] = jnp.sum(across, axis=1)
                return 0

            lax.fori_loop(0, columns // 256, chunk, 0)
            if it == 0 and s == 0:
                pl.semaphore_wait(barrier, has_low.astype(jnp.int32) + has_high.astype(jnp.int32))

            for way, there in sends:

                @pl.when(there)
                def _(way=way, s=s):
                    line_copy(it, way, s).start()

        for s in range(own):
            for way, there in receives:

                @pl.when(there)
                def _(way=way, s=s):
                    line_copy(it, way, s).wait_recv()

        for j in range(window):
            at = jnp.clip(first + j, 0, 3 * own - 1) * tiles + tiles_ref[0, j]
            line_rows[j] = jnp.where(j < number, lines[it, at], 0.0)
        for m in range(mats):
            x = line_rows[:, m, :]
            line_pack[m] = jnp.concatenate([x[:, :half], x[:, half:]], axis=0)

        def poisson(i, _):
            cols = pl.ds(pl.multiple_of(i * 128, 128), 128)
            xs = [line_pack[m, :, cols] for m in range(mats)]
            trans = []
            for k in range(energies):
                total = atten_ref[0, k] * xs[0]
                for m in range(1, mats):
                    total = total + atten_ref[m, k] * xs[m]
                trans.append(jnp.exp(-total))
            back = [None] * energies
            for e in range(bins):
                expected = spec_ref[e, 0] * trans[0]
                for k in range(1, energies):
                    expected = expected + spec_ref[e, k] * trans[k]
                weight = 1.0 - count_pack[e, :, cols] / expected
                for k in range(energies):
                    term = spec_ref[e, k] * weight
                    back[k] = term if e == 0 else back[k] + term
            for m in range(mats):
                total = None
                for k in range(energies):
                    term = atten_ref[m, k] * (trans[k] * back[k])
                    total = term if k == 0 else total + term
                grad_pack[m, :, cols] = -total
            return 0

        lax.fori_loop(0, half // 128, poisson, 0)
        for m in range(mats):
            y = grad_pack[m]
            grad_rows[:, m, :] = jnp.concatenate([y[:window], y[window:]], axis=1)
        for place in list(range(own)) + list(range(2 * own, 3 * own)) + list(range(own, 2 * own)):
            j = place - first
            held = (j >= 0) & (j < number)
            j = jnp.clip(j, 0, window - 1)
            value = grad_rows[j]
            tile = tiles_ref[0, j]
            for t in range(tiles):
                grad_send[it, place * tiles + t] = jnp.where(held & (tile == t), value, 0.0).astype(BF16)
        for way, there in sends:

            @pl.when(there)
            def _(way=way):
                grad_copy(it, way).start()

        for way, there in receives:

            @pl.when(there)
            def _(way=way):
                grad_copy(it, way).wait_recv()

        grad_sum[...] = (
            grad_send[it, pairs : 2 * pairs].astype(F32)
            + grad_recv[it, 0].astype(F32)
            + grad_recv[it, 1].astype(F32)
        )

        if it < ITERS - 1:

            def back_step(s, _):
                total = back_projected(mats, tiles, s, grad_sum, row, column)
                for m in range(mats):
                    new = maps[s, m] - step_ref[m] * total[m * height : (m + 1) * height]
                    maps[s, m] = new
                    rounded[s, m] = new.astype(BF16)
                return 0

            lax.fori_loop(0, own, back_step, 0)
            if it == ITERS - 2:
                for s in range(own):
                    maps_store(s).start()

    for s in range(own):
        maps_store(s).wait()
    for it in range(ITERS):
        for way, there in sends:

            @pl.when(there)
            def _(way=way, it=it):
                for s in range(own):
                    line_copy(it, way, s).wait_send()
                grad_copy(it, way).wait_send()


def solution(mesh):
    n = mesh.shape["view"]

    def local(materials, column_profile, row_profile, start, count, tile_ids, counts, spectrum, attenuation, step):
        mats, own, height, width = materials.shape
        tiles, _, columns = column_profile.shape
        views, window = tile_ids.shape
        bins = spectrum.shape[0]
        assert views == 1
        pairs = own * tiles
        vmem = pl.BlockSpec(memory_space=pltpu.VMEM)
        smem = pl.BlockSpec(memory_space=pltpu.SMEM)
        anywhere = pl.BlockSpec(memory_space=pl.ANY)
        grads, maps = pl.pallas_call(
            functools.partial(kernel, n),
            out_shape=[
                jax.ShapeDtypeStruct((pairs, mats, columns), F32),
                jax.ShapeDtypeStruct(materials.shape, F32),
            ],
            in_specs=[smem] * 6 + [anywhere] * 3 + [vmem],
            out_specs=[vmem, anywhere],
            scratch_shapes=[
                pltpu.VMEM((own, mats, height, width), F32),
                pltpu.VMEM(column_profile.shape, BF16),
                pltpu.VMEM(row_profile.shape, BF16),
                pltpu.VMEM((own, mats, height, width), BF16),
                pltpu.VMEM((ITERS, 3 * pairs, mats, columns), F32),
                pltpu.VMEM((window, mats, columns), F32),
                pltpu.VMEM((mats, 2 * window, columns // 2), F32),
                pltpu.VMEM((bins, 2 * window, columns // 2), F32),
                pltpu.VMEM((mats, 2 * window, columns // 2), F32),
                pltpu.VMEM((window, mats, columns), F32),
                pltpu.VMEM((ITERS, 3 * pairs, mats, columns), BF16),
                pltpu.VMEM((ITERS, 2, pairs, mats, columns), BF16),
                pltpu.SemaphoreType.DMA((own,)),
                pltpu.SemaphoreType.DMA((2, columns // 256)),
                pltpu.SemaphoreType.DMA((own,)),
                pltpu.SemaphoreType.DMA((ITERS, 2, own)),
                pltpu.SemaphoreType.DMA((ITERS, 2, own)),
                pltpu.SemaphoreType.DMA((ITERS, 2)),
                pltpu.SemaphoreType.DMA((ITERS, 2)),
            ],
            compiler_params=pltpu.CompilerParams(
                collective_id=0, has_side_effects=True, vmem_limit_bytes=56 * 1024 * 1024
            ),
        )(start, count, tile_ids, spectrum, attenuation.T, step, materials, column_profile, row_profile, counts)
        slab = pl.BlockSpec((mats, 1, height, width), lambda s: (0, s, 0, 0))
        return pl.pallas_call(
            final_kernel,
            grid=(own,),
            out_shape=jax.ShapeDtypeStruct(materials.shape, F32),
            in_specs=[smem, vmem, vmem, vmem, slab],
            out_specs=slab,
            compiler_params=pltpu.CompilerParams(vmem_limit_bytes=56 * 1024 * 1024),
        )(step, grads, column_profile, row_profile, maps)

    placed = (
        P(None, ("groups", "view"), None, None),
        P(),
        P(),
        P(("groups", "view")),
        P(("groups", "view")),
        P(("groups", "view"), None),
        P(("groups", "view"), None, None, None),
        P(),
        P(),
        P(),
    )
    return jax.shard_map(
        local,
        mesh=mesh,
        in_specs=placed,
        out_specs=P(None, ("groups", "view"), None, None),
        check_vma=False,
    )
```

```python
import functools

import jax
import jax.numpy as jnp
from jax import lax
from jax.experimental import pallas as pl
from jax.experimental.pallas import tpu as pltpu
from jax.sharding import PartitionSpec as P

ITERS = 2
MESH = pl.DeviceIdType.MESH
F32 = jnp.float32
BF16 = jnp.bfloat16


def back_projected(mats, tiles, s, grad_ref, row_ref, col_ref):
    total = None
    for t in range(tiles):
        g = grad_ref[s * tiles + t]
        profile = row_ref[t].astype(F32)
        weighted = jnp.concatenate([(g[m : m + 1] * profile).astype(BF16) for m in range(mats)], axis=0)
        part = lax.dot_general(weighted, col_ref[t], (((1,), (1,)), ((), ())), preferred_element_type=F32)
        total = part if t == 0 else total + part
    return total


def final_kernel(
    step_ref, grad_ref, col_ref, row_ref, mats_ref, out_ref, column, row, maps, new, tile_sem, load_sem, store_sem
):
    mats, own, height, _ = mats_ref.shape
    tiles = col_ref.shape[0]
    loads = [
        (
            pltpu.make_async_copy(row_ref.at[t], row.at[t], tile_sem.at[0, t]),
            pltpu.make_async_copy(col_ref.at[t], column.at[t], tile_sem.at[1, t]),
        )
        for t in range(tiles)
    ]
    slices = [pltpu.make_async_copy(mats_ref.at[:, s], maps.at[s], load_sem.at[s]) for s in range(own)]
    stores = [
        [pltpu.make_async_copy(new.at[s, m], out_ref.at[m, s], store_sem.at[s, m]) for m in range(mats)]
        for s in range(own)
    ]
    for pair in loads:
        for copy in pair:
            copy.start()
    for copy in slices:
        copy.start()
    for s in range(own):
        total = None
        for t in range(tiles):
            if s == 0:
                for copy in loads[t]:
                    copy.wait()
            g = grad_ref[s * tiles + t]
            profile = row[t].astype(F32)
            weighted = jnp.concatenate([(g[m : m + 1] * profile).astype(BF16) for m in range(mats)], axis=0)
            part = lax.dot_general(weighted, column[t], (((1,), (1,)), ((), ())), preferred_element_type=F32)
            total = part if t == 0 else total + part
        slices[s].wait()
        for m in range(mats):
            new[s, m] = maps[s, m] - step_ref[m] * total[m * height : (m + 1) * height]
            stores[s][m].start()
    for group in stores:
        for copy in group:
            copy.wait()


def kernel(
    n,
    start_ref,
    count_ref,
    tiles_ref,
    spec_ref,
    atten_ref,
    step_ref,
    mats_ref,
    col_ref,
    row_ref,
    counts_ref,
    grad_sum,
    mats_out,
    maps,
    column,
    row,
    rounded,
    lines,
    line_rows,
    line_pack,
    count_pack,
    grad_pack,
    grad_rows,
    grad_send,
    grad_recv,
    load_sem,
    chunk_sem,
    store_sem,
    line_send_sem,
    line_recv_sem,
    grad_send_sem,
    grad_recv_sem,
):
    me = lax.axis_index("view")
    mats, own, height, width = mats_ref.shape
    tiles, _, columns = col_ref.shape
    window = tiles_ref.shape[1]
    bins, energies = spec_ref.shape
    pairs = own * tiles
    half = columns // 2
    has_low, has_high = me > 0, me < n - 1
    low, high = jnp.maximum(me - 1, 0), jnp.minimum(me + 1, n - 1)

    def maps_load(s):
        return pltpu.make_async_copy(mats_ref.at[:, s], maps.at[s], load_sem.at[s])

    def chunk_load(which, i):
        cols = pl.ds(pl.multiple_of(i * 256, 256), 256)
        source, target = ((col_ref, column), (row_ref, row))[which]
        return pltpu.make_async_copy(source.at[:, :, cols], target.at[:, :, cols], chunk_sem.at[which, i])

    def maps_store(s):
        return pltpu.make_async_copy(maps.at[s], mats_out.at[:, s], store_sem.at[s])

    maps_load(0).start()
    for i in range(columns // 256):
        chunk_load(0, i).start()
        chunk_load(1, i).start()
    for s in range(1, own):
        maps_load(s).start()

    barrier = pltpu.get_barrier_semaphore()

    @pl.when(has_low)
    def _():
        pl.semaphore_signal(barrier, inc=1, device_id={"view": low}, device_id_type=MESH)

    @pl.when(has_high)
    def _():
        pl.semaphore_signal(barrier, inc=1, device_id={"view": high}, device_id_type=MESH)

    @pl.when(jnp.logical_not(has_low))
    def _():
        for it in range(ITERS):
            grad_recv[it, 0] = jnp.zeros(grad_recv.shape[2:], BF16)
            lines[it, 0:pairs] = jnp.zeros((pairs, mats, columns), F32)

    @pl.when(jnp.logical_not(has_high))
    def _():
        for it in range(ITERS):
            grad_recv[it, 1] = jnp.zeros(grad_recv.shape[2:], BF16)
            lines[it, 2 * pairs : 3 * pairs] = jnp.zeros((pairs, mats, columns), F32)

    def line_copy(it, way, s):
        landing = 0 if way == 0 else 2 * pairs
        return pltpu.make_async_remote_copy(
            src_ref=lines.at[it, pl.ds(pairs + s * tiles, tiles)],
            dst_ref=lines.at[it, pl.ds(landing + s * tiles, tiles)],
            send_sem=line_send_sem.at[it, way, s],
            recv_sem=line_recv_sem.at[it, way, s],
            device_id={"view": high if way == 0 else low},
            device_id_type=MESH,
        )

    def grad_copy(it, way):
        leaving = 2 * pairs if way == 0 else 0
        return pltpu.make_async_remote_copy(
            src_ref=grad_send.at[it, pl.ds(leaving, pairs)],
            dst_ref=grad_recv.at[it, way],
            send_sem=grad_send_sem.at[it, way],
            recv_sem=grad_recv_sem.at[it, way],
            device_id={"view": high if way == 0 else low},
            device_id_type=MESH,
        )

    sends = ((0, has_high), (1, has_low))
    receives = ((0, has_low), (1, has_high))

    for e in range(bins):
        c = counts_ref[0, e].astype(F32)
        count_pack[e] = jnp.concatenate([c[:, :half], c[:, half:]], axis=0)

    first = start_ref[0] - (me * own - own)
    number = count_ref[0]

    for it in range(ITERS):
        for s in range(own):
            if it == 0:
                maps_load(s).wait()
                for m in range(mats):
                    rounded[s, m] = maps[s, m].astype(BF16)

            def chunk(i, _, s=s):
                if it == 0 and s == 0:
                    chunk_load(0, i).wait()
                    chunk_load(1, i).wait()
                cols = pl.ds(pl.multiple_of(i * 256, 256), 256)
                block = rounded[s].reshape(mats * height, width)
                for t in range(tiles):
                    across = jnp.dot(block, column[t, :, cols], preferred_element_type=F32)
                    across = across.reshape(mats, height, 256) * row[t, :, cols].astype(F32)[None]
                    lines[it, pairs + s * tiles + t, :, cols] = jnp.sum(across, axis=1)
                return 0

            lax.fori_loop(0, columns // 256, chunk, 0, unroll=it > 0 or s > 0)
            if it == 0 and s == 0:
                pl.semaphore_wait(barrier, has_low.astype(jnp.int32) + has_high.astype(jnp.int32))

            for way, there in sends:

                @pl.when(there)
                def _(way=way, s=s):
                    line_copy(it, way, s).start()

        for s in range(own):
            for way, there in receives:

                @pl.when(there)
                def _(way=way, s=s):
                    line_copy(it, way, s).wait_recv()

        for j in range(window):
            at = jnp.clip(first + j, 0, 3 * own - 1) * tiles + tiles_ref[0, j]
            line_rows[j] = jnp.where(j < number, lines[it, at], 0.0)
        for m in range(mats):
            x = line_rows[:, m, :]
            line_pack[m] = jnp.concatenate([x[:, :half], x[:, half:]], axis=0)

        def poisson(i, _):
            cols = pl.ds(pl.multiple_of(i * 128, 128), 128)
            xs = [line_pack[m, :, cols] for m in range(mats)]
            trans = []
            for k in range(energies):
                total = atten_ref[0, k] * xs[0]
                for m in range(1, mats):
                    total = total + atten_ref[m, k] * xs[m]
                trans.append(jnp.exp(-total))
            back = [None] * energies
            for e in range(bins):
                expected = spec_ref[e, 0] * trans[0]
                for k in range(1, energies):
                    expected = expected + spec_ref[e, k] * trans[k]
                weight = 1.0 - count_pack[e, :, cols] / expected
                for k in range(energies):
                    term = spec_ref[e, k] * weight
                    back[k] = term if e == 0 else back[k] + term
            for m in range(mats):
                total = None
                for k in range(energies):
                    term = atten_ref[m, k] * (trans[k] * back[k])
                    total = term if k == 0 else total + term
                grad_pack[m, :, cols] = -total
            return 0

        lax.fori_loop(0, half // 128, poisson, 0, unroll=True)
        for m in range(mats):
            y = grad_pack[m]
            grad_rows[:, m, :] = jnp.concatenate([y[:window], y[window:]], axis=1)
        for place in list(range(own)) + list(range(2 * own, 3 * own)) + list(range(own, 2 * own)):
            j = place - first
            held = (j >= 0) & (j < number)
            j = jnp.clip(j, 0, window - 1)
            value = grad_rows[j]
            tile = tiles_ref[0, j]
            for t in range(tiles):
                grad_send[it, place * tiles + t] = jnp.where(held & (tile == t), value, 0.0).astype(BF16)
        for way, there in sends:

            @pl.when(there)
            def _(way=way):
                grad_copy(it, way).start()

        for way, there in receives:

            @pl.when(there)
            def _(way=way):
                grad_copy(it, way).wait_recv()

        grad_sum[...] = (
            grad_send[it, pairs : 2 * pairs].astype(F32)
            + grad_recv[it, 0].astype(F32)
            + grad_recv[it, 1].astype(F32)
        )

        if it < ITERS - 1:

            def back_step(s, _):
                total = back_projected(mats, tiles, s, grad_sum, row, column)
                for m in range(mats):
                    new = maps[s, m] - step_ref[m] * total[m * height : (m + 1) * height]
                    maps[s, m] = new
                    rounded[s, m] = new.astype(BF16)
                return 0

            lax.fori_loop(0, own, back_step, 0)
            if it == ITERS - 2:
                for s in range(own):
                    maps_store(s).start()

    for s in range(own):
        maps_store(s).wait()
    for it in range(ITERS):
        for way, there in sends:

            @pl.when(there)
            def _(way=way, it=it):
                for s in range(own):
                    line_copy(it, way, s).wait_send()
                grad_copy(it, way).wait_send()


def solution(mesh):
    n = mesh.shape["view"]

    def local(materials, column_profile, row_profile, start, count, tile_ids, counts, spectrum, attenuation, step):
        mats, own, height, width = materials.shape
        tiles, _, columns = column_profile.shape
        views, window = tile_ids.shape
        bins = spectrum.shape[0]
        assert views == 1
        pairs = own * tiles
        vmem = pl.BlockSpec(memory_space=pltpu.VMEM)
        smem = pl.BlockSpec(memory_space=pltpu.SMEM)
        anywhere = pl.BlockSpec(memory_space=pl.ANY)
        grads, maps = pl.pallas_call(
            functools.partial(kernel, n),
            out_shape=[
                jax.ShapeDtypeStruct((pairs, mats, columns), F32),
                jax.ShapeDtypeStruct(materials.shape, F32),
            ],
            in_specs=[smem] * 6 + [anywhere] * 3 + [vmem],
            out_specs=[vmem, anywhere],
            scratch_shapes=[
                pltpu.VMEM((own, mats, height, width), F32),
                pltpu.VMEM(column_profile.shape, BF16),
                pltpu.VMEM(row_profile.shape, BF16),
                pltpu.VMEM((own, mats, height, width), BF16),
                pltpu.VMEM((ITERS, 3 * pairs, mats, columns), F32),
                pltpu.VMEM((window, mats, columns), F32),
                pltpu.VMEM((mats, 2 * window, columns // 2), F32),
                pltpu.VMEM((bins, 2 * window, columns // 2), F32),
                pltpu.VMEM((mats, 2 * window, columns // 2), F32),
                pltpu.VMEM((window, mats, columns), F32),
                pltpu.VMEM((ITERS, 3 * pairs, mats, columns), BF16),
                pltpu.VMEM((ITERS, 2, pairs, mats, columns), BF16),
                pltpu.SemaphoreType.DMA((own,)),
                pltpu.SemaphoreType.DMA((2, columns // 256)),
                pltpu.SemaphoreType.DMA((own,)),
                pltpu.SemaphoreType.DMA((ITERS, 2, own)),
                pltpu.SemaphoreType.DMA((ITERS, 2, own)),
                pltpu.SemaphoreType.DMA((ITERS, 2)),
                pltpu.SemaphoreType.DMA((ITERS, 2)),
            ],
            compiler_params=pltpu.CompilerParams(
                collective_id=0, has_side_effects=True, vmem_limit_bytes=56 * 1024 * 1024
            ),
        )(start, count, tile_ids, spectrum, attenuation.T, step, materials, column_profile, row_profile, counts)
        return pl.pallas_call(
            final_kernel,
            out_shape=jax.ShapeDtypeStruct(materials.shape, F32),
            in_specs=[smem, vmem, anywhere, anywhere, anywhere],
            out_specs=anywhere,
            scratch_shapes=[
                pltpu.VMEM(column_profile.shape, BF16),
                pltpu.VMEM(row_profile.shape, BF16),
                pltpu.VMEM((own, mats, height, width), F32),
                pltpu.VMEM((own, mats, height, width), F32),
                pltpu.SemaphoreType.DMA((2, tiles)),
                pltpu.SemaphoreType.DMA((own,)),
                pltpu.SemaphoreType.DMA((own, mats)),
            ],
            compiler_params=pltpu.CompilerParams(vmem_limit_bytes=56 * 1024 * 1024),
        )(step, grads, column_profile, row_profile, maps)

    placed = (
        P(None, ("groups", "view"), None, None),
        P(),
        P(),
        P(("groups", "view")),
        P(("groups", "view")),
        P(("groups", "view"), None),
        P(("groups", "view"), None, None, None),
        P(),
        P(),
        P(),
    )
    return jax.shard_map(
        local,
        mesh=mesh,
        in_specs=placed,
        out_specs=P(None, ("groups", "view"), None, None),
        check_vma=False,
    )
```
